32 devices in a mesh: groups: 2 (over x), right: 4 (over y, core), left: 4 (over z).
Axes of the slice: x: 2, y: 2, z: 4, core: 2. Of those that a mesh axis runs over, the one named last changes fastest.
Arguments:
- left_act: bfloat16 [4096, 8192], P(('groups', 'right'), 'left'), parts along dimension 0, may hold values from -15 to 15
- right_act: bfloat16 [4096, 4096], P(('groups', 'left'), 'right'), parts along dimension 0, may hold values from -15 to 15
- counts: int32 [512, 128], P(('groups', 'left'), 'right'), parts along dimension 0, may hold values from 512 to 2048
- w_out: bfloat16 [1024, 128], replicated, may hold values from -0.1875 to 0.1875
Outputs:
- pair_update: float32 [512, 128, 128], P(('groups', 'left'), 'right'), parts along dimension 0
The draws below stay inside these ranges and needn't reach their ends.
There are 2 independent parts, one for each index of `groups`. The reference program is written for one: setup_inputs(seed, part) draws one part's arguments, and reference() takes and returns one part's arrays. A program takes and returns all parts, laid end to end along the dimension named above; an argument that names none is the same for every part. Nothing has to cross between parts.
All inputs are finite; a program needn't handle non-finite values.
Results may differ from the reference program's by a relative error of at most 0.0029.
Values may be sent and summed in bfloat16 or wider, within the bound.
A program may use at most 128 MiB of HBM per device.

```python
import jax
import jax.numpy as jnp
from jax import lax

CH = 32
PAIR = 128
SEQS = 2048
LEFT = 256
RIGHT = 128


def place_ends(array, key, smallest, top_value):
    longest = array.shape.index(max(array.shape))
    spots = []
    for shift in (0, 1):
        where = [jax.random.randint(jax.random.fold_in(key, axis), (), 0, length) for axis, length in enumerate(array.shape)]
        where[longest] = (where[longest] + shift) % array.shape[longest]
        spots.append(tuple(where))
    return array.at[spots[0]].set(smallest).at[spots[1]].set(top_value)


def shard_levels(key, dims, pieces, least, largest):
    level, own = 1.0, jax.random.fold_in(key, 6)
    for position, shards_of in pieces:
        heights = jnp.exp(jax.random.uniform(jax.random.fold_in(own, position), (shards_of,), jnp.float32, least / len(pieces), largest / len(pieces)))
        level = level * jnp.repeat(heights, dims[position] // shards_of).reshape([-1 if axis == position else 1 for axis in range(len(dims))])
    return level


def bell_draw(rng, dims, spread, most, split=(), kind=jnp.bfloat16):
    values = jax.random.normal(rng, dims, jnp.float32) * spread
    if len(split) > 0:
        values = shard_levels(rng, dims, split, -0.22, 0.18) * values
    return jnp.clip(values, min=-most, max=most).astype(kind)


def setup_inputs(seed: int = 0, part: int = 0) -> dict:
    splits = jax.random.split(jax.random.key(seed), 5)
    own_keys = jax.random.split(jax.random.fold_in(splits[4], part), 5)
    left_act = bell_draw(own_keys[0], (SEQS, LEFT * CH), 3.0, 15.0, ((0, 4), (1, 4)))
    right_act = bell_draw(own_keys[1], (SEQS, RIGHT * CH), 3.0, 15.0, ((0, 4), (1, 4)))
    counts = place_ends(jax.random.randint(own_keys[2], (LEFT, RIGHT), SEQS // 4, SEQS + 1), jax.random.fold_in(own_keys[2], 1), SEQS // 4, SEQS).astype(jnp.int32)
    w_out = bell_draw(splits[3], (CH * CH, PAIR), (CH * CH) ** -0.5, 0.1875)
    return dict(left_act=left_act, right_act=right_act, counts=counts, w_out=w_out)


def reference(left_act, right_act, counts, w_out):
    block = 16 if LEFT % 16 == 0 else 2
    width = block * CH

    def one_block(index):
        columns = lax.dynamic_slice_in_dim(left_act, (index * width).astype(jnp.int32), width, 1)
        outer = lax.dot_general(columns, right_act, (((0,), (0,)), ((), ())), preferred_element_type=jnp.float32)
        outer = outer.reshape(block, CH, RIGHT, CH).transpose(0, 2, 1, 3).reshape(block * RIGHT, CH * CH)
        flat = outer.astype(jnp.bfloat16)
        projected = jnp.dot(flat, w_out, preferred_element_type=jnp.float32).reshape(block, RIGHT, PAIR)
        cover = lax.dynamic_slice_in_dim(counts, (index * block).astype(jnp.int32), block, 0)
        return projected / cover.astype(jnp.float32)[:, :, None]

    blocks = lax.map(one_block, jnp.arange(LEFT // block, dtype=jnp.int32))
    return blocks.reshape(LEFT, RIGHT, PAIR)
```

```python
import functools

import jax
import jax.numpy as jnp
from jax import lax
from jax.experimental import pallas as pl
from jax.experimental.pallas import tpu as pltpu
from jax.sharding import PartitionSpec as P

CH = 32
CORES = 2
MESH = pl.DeviceIdType.MESH


def lane_quads(tiles):
    lane = lax.broadcasted_iota(jnp.int32, tiles[0].shape, 1)
    low = lane < 64
    even = (lane % 64) < 32
    stage = [None] * 4
    for c in range(2):
        a, b = tiles[c], tiles[c + 2]
        stage[c] = jnp.where(low, a, pltpu.roll(b, 64, 1))
        stage[c + 2] = jnp.where(low, pltpu.roll(a, 64, 1), b)
    outs = [None] * 4
    for half in range(2):
        a, b = stage[2 * half], stage[2 * half + 1]
        outs[2 * half] = jnp.where(even, a, pltpu.roll(b, 32, 1))
        outs[2 * half + 1] = jnp.where(even, pltpu.roll(a, 96, 1), b)
    return outs


def kernel(sizes, left_ref, right_ref, w_ref, out_ref, left_full, right_full, left_t, acc, flat,
           z_send, z_recv, y_send, y_recv, s_send, s_recv, own_sem):
    n_z, n_r, q_z, q_y = sizes
    n_y = n_r // CORES
    rows_l, width_l = left_ref.shape
    rows_r, width_r = right_ref.shape
    piece_r = width_r // q_z
    piece_l = rows_l // q_y
    left_dev = width_l // CH
    right_dev = width_r // CH
    seqs = left_t.shape[1]
    z = lax.axis_index("left")
    r = lax.axis_index("right")
    y = r // CORES
    k = r % CORES

    def z_dev(pos):
        return {"left": pos}

    def y_dev(pos):
        return {"right": pos * CORES + k}

    sib_dev = {"right": y * CORES + (1 - k)}

    barrier = pltpu.get_barrier_semaphore()

    def greet(dev):
        pl.semaphore_signal(barrier, inc=1, device_id=dev, device_id_type=MESH)

    greet(sib_dev)
    for pos, n, dev in ((z, n_z, z_dev), (y, n_y, y_dev)):
        pl.when(pos + 1 < n)(functools.partial(greet, dev(pos + 1)))
        pl.when(pos >= 1)(functools.partial(greet, dev(pos - 1)))
    total = 1 + (z + 1 < n_z).astype(jnp.int32) + (z >= 1).astype(jnp.int32)
    total = total + (y + 1 < n_y).astype(jnp.int32) + (y >= 1).astype(jnp.int32)
    pl.semaphore_wait(barrier, total)

    def z_slot(chunk, q):
        return right_full.at[pl.ds(pl.multiple_of(chunk * rows_r, rows_r), rows_r), pl.ds(q * piece_r, piece_r)]

    def z_copy(side, step, q):
        sign = 1 - 2 * side
        chunk = z - sign * step
        src = right_ref.at[:, pl.ds(q * piece_r, piece_r)] if step == 0 else z_slot(chunk, q)
        at = step * q_z + q
        return pltpu.make_async_remote_copy(
            src_ref=src, dst_ref=z_slot(chunk, q), send_sem=z_send.at[side, at], recv_sem=z_recv.at[side, at],
            device_id=z_dev(z + sign), device_id_type=MESH)

    def z_sends(side, step):
        near = z + 1 < n_z if side == 0 else z >= 1
        far = z - step >= 0 if side == 0 else z + step < n_z
        return jnp.logical_and(near, far)

    def z_arrives(side, step):
        return z - step - 1 >= 0 if side == 0 else z + step + 1 < n_z

    def z_wait(side, step, q):
        sign = 1 - 2 * side
        slot = z_slot(z - sign * (step + 1), q)
        pltpu.make_async_copy(slot, slot, z_recv.at[side, step * q_z + q]).wait()

    def l_slot(chunk, q):
        return left_full.at[pl.ds(pl.multiple_of(chunk * rows_l + q * piece_l, piece_l), piece_l), :]

    def l_own(q):
        return left_ref.at[pl.ds(q * piece_l, piece_l), :]

    def y_copy(side, step, q):
        sign = 1 - 2 * side
        chunk = (y - sign * step) * CORES + k
        at = step * q_y + q
        return pltpu.make_async_remote_copy(
            src_ref=l_own(q) if step == 0 else l_slot(chunk, q), dst_ref=l_slot(chunk, q),
            send_sem=y_send.at[side, at], recv_sem=y_recv.at[side, at],
            device_id=y_dev(y + sign), device_id_type=MESH)

    def y_sends(side, step):
        near = y + 1 < n_y if side == 0 else y >= 1
        far = y - step >= 0 if side == 0 else y + step < n_y
        return jnp.logical_and(near, far)

    def y_arrives(side, step):
        return y - step - 1 >= 0 if side == 0 else y + step + 1 < n_y

    def y_wait(side, step, q):
        sign = 1 - 2 * side
        slot = l_slot((y - sign * (step + 1)) * CORES + k, q)
        pltpu.make_async_copy(slot, slot, y_recv.at[side, step * q_y + q]).wait()

    def s_at(side, step, q):
        if step < 0:
            return q
        return (1 + side * (n_y - 1) + step) * q_y + q

    def s_copy(side, step, q):
        sign = 1 - 2 * side
        chunk = (y - sign * (step + 1)) * CORES + k if step >= 0 else r
        at = s_at(side, step, q)
        return pltpu.make_async_remote_copy(
            src_ref=l_own(q) if step < 0 else l_slot(chunk, q), dst_ref=l_slot(chunk, q),
            send_sem=s_send.at[at], recv_sem=s_recv.at[at],
            device_id=sib_dev, device_id_type=MESH)

    def s_wait(side, step, q):
        sign = 1 - 2 * side
        y_from = y - sign * (step + 1) if step >= 0 else y
        slot = l_slot(y_from * CORES + (1 - k), q)
        pltpu.make_async_copy(slot, slot, s_recv.at[s_at(side, step, q)]).wait()

    tile = 256

    def turn(src, first_row, chunk, q):
        col = pl.multiple_of(chunk * rows_l + q * piece_l, piece_l)

        def body(m, carry):
            at = pl.multiple_of(m * tile, tile)
            left_t[pl.ds(at, tile), pl.ds(col, piece_l)] = src[pl.ds(first_row, piece_l), pl.ds(at, tile)].T
            return carry

        lax.fori_loop(0, width_l // tile, body, 0)

    def turn_full(chunk, q):
        turn(left_full, pl.multiple_of(chunk * rows_l + q * piece_l, piece_l), chunk, q)

    own = pltpu.make_async_copy(right_ref, right_full.at[pl.ds(pl.multiple_of(z * rows_r, rows_r), rows_r), :], own_sem)
    own.start()
    for q in range(max(q_z, q_y)):
        for side in range(2):
            if q < q_z:
                pl.when(z_sends(side, 0))(lambda side=side, q=q: z_copy(side, 0, q).start())
            if q < q_y:
                pl.when(y_sends(side, 0))(lambda side=side, q=q: y_copy(side, 0, q).start())
    for q in range(q_y):
        s_copy(0, -1, q).start()
    for q in range(q_y):
        turn(left_ref, q * piece_l, r, q)
    for q in range(q_y):
        s_wait(0, -1, q)
        turn_full(y * CORES + (1 - k), q)

    def z_tick(step, q):
        for side in range(2):
            @pl.when(z_arrives(side, step))
            def _():
                z_wait(side, step, q)
                if step + 1 < n_z - 1:
                    pl.when(z_sends(side, step + 1))(lambda: z_copy(side, step + 1, q).start())

    def y_tick(step, q):
        for side in range(2):
            @pl.when(y_arrives(side, step))
            def _():
                y_wait(side, step, q)
                s_copy(side, step, q).start()
                if step + 1 < n_y - 1:
                    pl.when(y_sends(side, step + 1))(lambda: y_copy(side, step + 1, q).start())

        for side in range(2):
            @pl.when(y_arrives(side, step))
            def _():
                sign = 1 - 2 * side
                y_from = y - sign * (step + 1)
                turn_full(y_from * CORES + k, q)
                s_wait(side, step, q)
                turn_full(y_from * CORES + (1 - k), q)

    y_ticks = [(step, q) for step in range(n_y - 1) for q in range(q_y)]
    for t in range((n_z - 2) * q_z):
        z_tick(t // q_z, t % q_z)
        if t % 2 == 1 and y_ticks:
            y_tick(*y_ticks.pop(0))
    for tick in y_ticks:
        y_tick(*tick)
    own.wait()

    block = 512
    at_end = jnp.logical_or(z == 0, z == n_z - 1)
    base = jnp.where(z == 0, 0, rows_r)
    base = pl.multiple_of(base, rows_r)

    def product(q, first, depth, add):
        cols = pl.ds(q * piece_r, piece_r)

        def body(m, carry):
            rows = pl.ds(pl.multiple_of(m * block, block), block)
            value = jnp.dot(left_t[rows, pl.ds(first, depth)], right_full[pl.ds(first, depth), cols],
                            preferred_element_type=jnp.float32)
            for part in range(piece_r // 128):
                some = value[:, part * 128:(part + 1) * 128]
                slab = q * (piece_r // 128) + part
                acc[slab, rows, :] = acc[slab, rows, :] + some if add else some
            return carry

        lax.fori_loop(0, width_l // block, body, 0)

    def first_part(q):
        @pl.when(at_end)
        def _():
            product(q, base, seqs - rows_r, False)

        @pl.when(jnp.logical_not(at_end))
        def _():
            product(q, 0, seqs, False)

    for q in range(q_z):
        first_part(q)

    def finish(q):
        heads = piece_r // CH
        for quad in range(heads // 4):
            slab = acc.at[q * (piece_r // 128) + quad]
            for cq in range(CH // 4):
                tiles = [slab[pl.ds(cq * 4 + c, left_dev, stride=CH), :] for c in range(4)]
                for j, value in enumerate(lane_quads(tiles)):
                    flat[pl.ds((quad * 4 + j) * left_dev, left_dev), pl.ds(cq * 128, 128)] = value.astype(jnp.bfloat16)
        projected = jnp.dot(flat[...], w_ref[...], preferred_element_type=jnp.float32)
        for j in range(heads):
            out_ref[pl.ds(q * heads + j, left_dev, stride=right_dev), :] = projected[j * left_dev:(j + 1) * left_dev, :]

    last = n_z - 2
    for q in range(q_z):
        z_tick(last, q)

        @pl.when(at_end)
        def _():
            far = jnp.where(z == 0, (n_z - 1) * rows_r, 0)
            product(q, pl.multiple_of(far, rows_r), rows_r, True)

        finish(q)

    for side in range(2):
        for step in range(n_z - 1):
            for q in range(q_z):
                pl.when(z_sends(side, step))(lambda side=side, step=step, q=q: z_copy(side, step, q).wait_send())
        for step in range(n_y - 1):
            for q in range(q_y):
                pl.when(y_sends(side, step))(lambda side=side, step=step, q=q: y_copy(side, step, q).wait_send())
                pl.when(y_arrives(side, step))(lambda side=side, step=step, q=q: s_copy(side, step, q).wait_send())
    for q in range(q_y):
        s_copy(0, -1, q).wait_send()


def solution(mesh):
    n_z, n_r = mesh.shape["left"], mesh.shape["right"]
    n_y = n_r // CORES

    def shards(left_act, right_act, counts, w_out):
        rows_l, width_l = left_act.shape
        rows_r, width_r = right_act.shape
        seqs = rows_r * n_z
        left_dev, right_dev = counts.shape
        pair = w_out.shape[1]
        q_z = width_r // 256
        q_y = rows_l // max(128, rows_l // 4)
        projected = pl.pallas_call(
            functools.partial(kernel, (n_z, n_r, q_z, q_y)),
            out_shape=jax.ShapeDtypeStruct((left_dev * right_dev, pair), jnp.float32),
            in_specs=[pl.BlockSpec(memory_space=pltpu.VMEM)] * 3,
            out_specs=pl.BlockSpec(memory_space=pltpu.VMEM),
            scratch_shapes=[
                pltpu.VMEM((seqs, width_l), jnp.bfloat16),
                pltpu.VMEM((seqs, width_r), jnp.bfloat16),
                pltpu.VMEM((width_l, seqs), jnp.bfloat16),
                pltpu.VMEM((width_r // 128, width_l, 128), jnp.float32),
                pltpu.VMEM((width_r // q_z // CH * left_dev, CH * CH), jnp.bfloat16),
                pltpu.SemaphoreType.DMA((2, (n_z - 1) * q_z)),
                pltpu.SemaphoreType.DMA((2, (n_z - 1) * q_z)),
                pltpu.SemaphoreType.DMA((2, (n_y - 1) * q_y)),
                pltpu.SemaphoreType.DMA((2, (n_y - 1) * q_y)),
                pltpu.SemaphoreType.DMA(((2 * n_y - 1) * q_y,)),
                pltpu.SemaphoreType.DMA(((2 * n_y - 1) * q_y,)),
                pltpu.SemaphoreType.DMA,
            ],
            compiler_params=pltpu.CompilerParams(
                collective_id=0, has_side_effects=True, vmem_limit_bytes=56 * 1024 * 1024
            ),
            name="pair_mean",
        )(left_act, right_act, w_out)
        projected = projected.reshape(left_dev, right_dev, pair)
        return projected / counts.astype(jnp.float32)[:, :, None]

    in_specs = (
        P(("groups", "right"), "left"),
        P(("groups", "left"), "right"),
        P(("groups", "left"), "right"),
        P(),
    )
    out_specs = P(("groups", "left"), "right", None)
    return jax.shard_map(shards, mesh=mesh, in_specs=in_specs, out_specs=out_specs, check_vma=False)
```

```python
import functools

import jax
import jax.numpy as jnp
from jax import lax
from jax.experimental import pallas as pl
from jax.experimental.pallas import tpu as pltpu
from jax.sharding import PartitionSpec as P

CH = 32
CORES = 2
MESH = pl.DeviceIdType.MESH


def lane_quads(tiles):
    lane = lax.broadcasted_iota(jnp.int32, tiles[0].shape, 1)
    low = lane < 64
    even = (lane % 64) < 32
    stage = [None] * 4
    for c in range(2):
        a, b = tiles[c], tiles[c + 2]
        stage[c] = jnp.where(low, a, pltpu.roll(b, 64, 1))
        stage[c + 2] = jnp.where(low, pltpu.roll(a, 64, 1), b)
    outs = [None] * 4
    for half in range(2):
        a, b = stage[2 * half], stage[2 * half + 1]
        outs[2 * half] = jnp.where(even, a, pltpu.roll(b, 32, 1))
        outs[2 * half + 1] = jnp.where(even, pltpu.roll(a, 96, 1), b)
    return outs


def kernel(sizes, left_ref, right_ref, w_ref, out_ref, left_full, right_full, left_t, acc, flat,
           z_send, z_recv, y_send, y_recv, s_send, s_recv, own_sem, *extra):
    n_z, n_r, q_z, q_y = sizes
    lends = len(extra) > 0
    if lends:
        lent, lent_t, part_out, part_in, ready, l_send, l_recv, ls_send, ls_recv, p_send, p_recv = extra
    n_y = n_r // CORES
    rows_l, width_l = left_ref.shape
    rows_r, width_r = right_ref.shape
    piece_r = width_r // q_z
    piece_l = rows_l // q_y
    left_dev = width_l // CH
    right_dev = width_r // CH
    seqs = left_t.shape[1]
    z = lax.axis_index("left")
    r = lax.axis_index("right")
    y = r // CORES
    k = r % CORES

    def z_dev(pos):
        return {"left": pos}

    def y_dev(pos):
        return {"right": pos * CORES + k}

    at_end = jnp.logical_or(z == 0, z == n_z - 1)
    at_helper = jnp.logical_not(at_end)
    moved = y + 1
    lender = jnp.where(z == 1, 0, n_z - 1)
    helper = jnp.where(z == 0, 1, n_z - 2)
    owner = r == moved
    half = jnp.where(owner, 1, 0)

    sib_dev = {"right": y * CORES + (1 - k)}

    barrier = pltpu.get_barrier_semaphore()

    def greet(dev):
        pl.semaphore_signal(barrier, inc=1, device_id=dev, device_id_type=MESH)

    greet(sib_dev)
    for pos, n, dev in ((z, n_z, z_dev), (y, n_y, y_dev)):
        pl.when(pos + 1 < n)(functools.partial(greet, dev(pos + 1)))
        pl.when(pos >= 1)(functools.partial(greet, dev(pos - 1)))
    total = 1 + (z + 1 < n_z).astype(jnp.int32) + (z >= 1).astype(jnp.int32)
    total = total + (y + 1 < n_y).astype(jnp.int32) + (y >= 1).astype(jnp.int32)
    pl.semaphore_wait(barrier, total)

    def z_slot(chunk, q):
        return right_full.at[pl.ds(pl.multiple_of(chunk * rows_r, rows_r), rows_r), pl.ds(q * piece_r, piece_r)]

    def z_copy(side, step, q):
        sign = 1 - 2 * side
        chunk = z - sign * step
        src = right_ref.at[:, pl.ds(q * piece_r, piece_r)] if step == 0 else z_slot(chunk, q)
        at = step * q_z + q
        return pltpu.make_async_remote_copy(
            src_ref=src, dst_ref=z_slot(chunk, q), send_sem=z_send.at[side, at], recv_sem=z_recv.at[side, at],
            device_id=z_dev(z + sign), device_id_type=MESH)

    def z_sends(side, step):
        near = z + 1 < n_z if side == 0 else z >= 1
        far = z - step >= 0 if side == 0 else z + step < n_z
        go = jnp.logical_and(near, far)
        if lends:
            sign = 1 - 2 * side
            kept = jnp.logical_and(z + sign == (n_z - 1 if side == 0 else 0), z - sign * step == moved)
            go = jnp.logical_and(go, jnp.logical_not(kept))
        return go

    def z_arrives(side, step):
        comes = z - step - 1 >= 0 if side == 0 else z + step + 1 < n_z
        if lends:
            sign = 1 - 2 * side
            kept = jnp.logical_and(at_end, z - sign * (step + 1) == moved)
            comes = jnp.logical_and(comes, jnp.logical_not(kept))
        return comes

    def z_wait(side, step, q):
        sign = 1 - 2 * side
        slot = z_slot(z - sign * (step + 1), q)
        pltpu.make_async_copy(slot, slot, z_recv.at[side, step * q_z + q]).wait()

    def l_slot(chunk, q):
        return left_full.at[pl.ds(pl.multiple_of(chunk * rows_l + q * piece_l, piece_l), piece_l), :]

    def l_own(q):
        return left_ref.at[pl.ds(q * piece_l, piece_l), :]

    def y_copy(side, step, q):
        sign = 1 - 2 * side
        chunk = (y - sign * step) * CORES + k
        at = step * q_y + q
        return pltpu.make_async_remote_copy(
            src_ref=l_own(q) if step == 0 else l_slot(chunk, q), dst_ref=l_slot(chunk, q),
            send_sem=y_send.at[side, at], recv_sem=y_recv.at[side, at],
            device_id=y_dev(y + sign), device_id_type=MESH)

    def y_sends(side, step):
        near = y + 1 < n_y if side == 0 else y >= 1
        far = y - step >= 0 if side == 0 else y + step < n_y
        return jnp.logical_and(near, far)

    def y_arrives(side, step):
        return y - step - 1 >= 0 if side == 0 else y + step + 1 < n_y

    def y_wait(side, step, q):
        sign = 1 - 2 * side
        slot = l_slot((y - sign * (step + 1)) * CORES + k, q)
        pltpu.make_async_copy(slot, slot, y_recv.at[side, step * q_y + q]).wait()

    def s_at(side, step, q):
        if step < 0:
            return q
        return (1 + side * (n_y - 1) + step) * q_y + q

    def s_copy(side, step, q):
        sign = 1 - 2 * side
        chunk = (y - sign * (step + 1)) * CORES + k if step >= 0 else r
        at = s_at(side, step, q)
        return pltpu.make_async_remote_copy(
            src_ref=l_own(q) if step < 0 else l_slot(chunk, q), dst_ref=l_slot(chunk, q),
            send_sem=s_send.at[at], recv_sem=s_recv.at[at],
            device_id=sib_dev, device_id_type=MESH)

    def s_wait(side, step, q):
        sign = 1 - 2 * side
        y_from = y - sign * (step + 1) if step >= 0 else y
        slot = l_slot(y_from * CORES + (1 - k), q)
        pltpu.make_async_copy(slot, slot, s_recv.at[s_at(side, step, q)]).wait()

    tile = 256

    def turn(src, first_row, chunk, q):
        col = pl.multiple_of(chunk * rows_l + q * piece_l, piece_l)

        def body(m, carry):
            at = pl.multiple_of(m * tile, tile)
            left_t[pl.ds(at, tile), pl.ds(col, piece_l)] = src[pl.ds(first_row, piece_l), pl.ds(at, tile)].T
            return carry

        lax.fori_loop(0, width_l // tile, body, 0)

    def turn_full(chunk, q):
        turn(left_full, pl.multiple_of(chunk * rows_l + q * piece_l, piece_l), chunk, q)

    own = pltpu.make_async_copy(right_ref, right_full.at[pl.ds(pl.multiple_of(z * rows_r, rows_r), rows_r), :], own_sem)
    own.start()
    def z_start():
        for q in range(q_z):
            for side in range(2):
                pl.when(z_sends(side, 0))(lambda side=side, q=q: z_copy(side, 0, q).start())

    def lent_rows(part, p):
        return pl.ds(pl.multiple_of(part * (rows_l // 2) + p * piece_l, piece_l), piece_l)

    def lend(p, from_own):
        base_row = pl.multiple_of(moved * rows_l + half * (rows_l // 2) + p * piece_l, piece_l)
        return pltpu.make_async_remote_copy(
            src_ref=left_ref.at[lent_rows(half, p), :] if from_own else left_full.at[pl.ds(base_row, piece_l), :],
            dst_ref=lent.at[lent_rows(half, p), :], send_sem=l_send.at[p], recv_sem=l_recv.at[p],
            device_id=z_dev(helper), device_id_type=MESH)

    def lent_across(p):
        slot = lent.at[lent_rows(half, p), :]
        return pltpu.make_async_remote_copy(
            src_ref=slot, dst_ref=slot, send_sem=ls_send.at[p], recv_sem=ls_recv.at[p],
            device_id=sib_dev, device_id_type=MESH)

    def part_copy(q):
        return pltpu.make_async_remote_copy(
            src_ref=part_out.at[q], dst_ref=part_in.at[q], send_sem=p_send.at[q], recv_sem=p_recv.at[q],
            device_id=z_dev(lender), device_id_type=MESH)

    lent_pieces = q_y // 2
    end_owner = jnp.logical_and(at_end, owner)
    end_other = jnp.logical_and(at_end, jnp.logical_not(owner))

    for q in range(q_y):
        s_copy(0, -1, q).start()
    for q in range(q_y):
        for side in range(2):
            pl.when(y_sends(side, 0))(lambda side=side, q=q: y_copy(side, 0, q).start())
    if lends:
        pl.when(at_helper)(z_start)

        @pl.when(end_owner)
        def _():
            for p in range(lent_pieces):
                lend(p, True).start()
            z_start()

        for p in range(lent_pieces):
            s_wait(0, -1, p)

        @pl.when(end_other)
        def _():
            for p in range(lent_pieces):
                lend(p, False).start()
            z_start()
    else:
        z_start()
    for q in range(q_y):
        turn(left_ref, q * piece_l, r, q)
    for q in range(q_y):
        if not lends or q >= lent_pieces:
            s_wait(0, -1, q)
        turn_full(y * CORES + (1 - k), q)

    def z_tick(step, q, only=None):
        for side in range(2):
            arrives = z_arrives(side, step)
            if only is not None:
                from_end = z == (1 if side == 0 else n_z - 2)
                arrives = jnp.logical_and(arrives, from_end if only else jnp.logical_not(from_end))

            @pl.when(arrives)
            def _():
                z_wait(side, step, q)
                if step + 1 < n_z - 1:
                    pl.when(z_sends(side, step + 1))(lambda: z_copy(side, step + 1, q).start())

    def y_tick(step, q):
        for side in range(2):
            @pl.when(y_arrives(side, step))
            def _():
                y_wait(side, step, q)
                s_copy(side, step, q).start()
                if step + 1 < n_y - 1:
                    pl.when(y_sends(side, step + 1))(lambda: y_copy(side, step + 1, q).start())

        for side in range(2):
            @pl.when(y_arrives(side, step))
            def _():
                sign = 1 - 2 * side
                y_from = y - sign * (step + 1)
                turn_full(y_from * CORES + k, q)
                s_wait(side, step, q)
                turn_full(y_from * CORES + (1 - k), q)

    block = 512
    base = jnp.where(z == 0, 0, rows_r)
    base = pl.multiple_of(base, rows_r)

    def product(q, terms, add):
        cols = pl.ds(q * piece_r, piece_r)

        def body(m, carry):
            rows = pl.ds(pl.multiple_of(m * block, block), block)
            value = None
            for turned, col, first, depth in terms:
                one = jnp.dot(turned[rows, pl.ds(col, depth)], right_full[pl.ds(first, depth), cols],
                              preferred_element_type=jnp.float32)
                value = one if value is None else value + one
            for part in range(piece_r // 128):
                some = value[:, part * 128:(part + 1) * 128]
                slab = q * (piece_r // 128) + part
                acc[slab, rows, :] = acc[slab, rows, :] + some if add else some
            return carry

        lax.fori_loop(0, width_l // block, body, 0)

    def chunk_term(chunk):
        first = pl.multiple_of(chunk * rows_r, rows_r)
        return (left_t, first, first, rows_r)

    heads = piece_r // CH

    def project(q):
        for quad in range(heads // 4):
            slab = acc.at[q * (piece_r // 128) + quad]
            for cq in range(CH // 4):
                tiles = [slab[pl.ds(cq * 4 + c, left_dev, stride=CH), :] for c in range(4)]
                for j, value in enumerate(lane_quads(tiles)):
                    flat[pl.ds((quad * 4 + j) * left_dev, left_dev), pl.ds(cq * 128, 128)] = value.astype(jnp.bfloat16)
        return jnp.dot(flat[...], w_ref[...], preferred_element_type=jnp.float32)

    def put(q, projected):
        for j in range(heads):
            out_ref[pl.ds(q * heads + j, left_dev, stride=right_dev), :] = projected[j * left_dev:(j + 1) * left_dev, :]

    y_ticks = [(step, q) for step in range(n_y - 1) for q in range(q_y)]
    if lends:
        def take_lent(p):
            slot = lent.at[lent_rows(half, p), :]
            pltpu.make_async_copy(slot, slot, l_recv.at[p]).wait()
            lent_across(p).start()

        def turn_lent(part, p):
            def body(m, carry):
                at = pl.multiple_of(m * tile, tile)
                lent_t[pl.ds(at, tile), lent_rows(part, p)] = lent[lent_rows(part, p), pl.ds(at, tile)].T
                return carry

            lax.fori_loop(0, width_l // tile, body, 0)

        def use_lent(p):
            turn_lent(half, p)
            slot = lent.at[lent_rows(1 - half, p), :]
            pltpu.make_async_copy(slot, slot, ls_recv.at[p]).wait()
            turn_lent(1 - half, p)

        for q in range(q_z):
            z_tick(0, q, only=False)
            if q % 2 == 1:
                y_tick(*y_ticks.pop(0))
                pl.when(at_helper)(functools.partial(take_lent, q // 2))
                pl.when(at_helper)(functools.partial(use_lent, q // 2))
        own.wait()
        for q in range(q_z):
            z_tick(0, q, only=True)
            z_tick(1, q)

            @pl.when(at_helper)
            def _():
                product(q, [(lent_t, 0, pl.multiple_of(moved * rows_r, rows_r), rows_r)], False)
                part_out[q] = project(q).astype(jnp.bfloat16)

            if q % 2 == 1:
                y_tick(*y_ticks.pop(0))

        @pl.when(at_helper)
        def _():
            for q in range(q_z):
                part_copy(q).start()

        for q in range(q_z):
            @pl.when(at_end)
            def _():
                product(q, [chunk_term(z), chunk_term(n_z - 1 - moved)], False)

            @pl.when(at_helper)
            def _():
                product(q, [(left_t, 0, 0, seqs)], False)
                put(q, project(q))

        @pl.when(at_end)
        def _():
            for q in range(q_z):
                z_tick(2, q)
                product(q, [chunk_term(n_z - 1 - z)], True)
                ready[q] = project(q)
            for q in range(q_z):
                slot = part_in.at[q]
                pltpu.make_async_copy(slot, slot, p_recv.at[q]).wait()
                put(q, ready[q] + part_in[q].astype(jnp.float32))
            for p in range(lent_pieces):
                lend(p, True).wait_send()

        @pl.when(at_helper)
        def _():
            for p in range(lent_pieces):
                lent_across(p).wait_send()
            for q in range(q_z):
                part_copy(q).wait_send()
    else:
        for t in range((n_z - 2) * q_z):
            z_tick(t // q_z, t % q_z)
            if t % 2 == 1 and y_ticks:
                y_tick(*y_ticks.pop(0))
        for tick in y_ticks:
            y_tick(*tick)
        own.wait()
        for q in range(q_z):
            @pl.when(at_end)
            def _():
                product(q, [(left_t, base, base, seqs - rows_r)], False)

            @pl.when(at_helper)
            def _():
                product(q, [(left_t, 0, 0, seqs)], False)
        for q in range(q_z):
            z_tick(n_z - 2, q)

            @pl.when(at_end)
            def _():
                product(q, [chunk_term(jnp.where(z == 0, n_z - 1, 0))], True)

            put(q, project(q))

    for side in range(2):
        for step in range(n_z - 1):
            for q in range(q_z):
                pl.when(z_sends(side, step))(lambda side=side, step=step, q=q: z_copy(side, step, q).wait_send())
        for step in range(n_y - 1):
            for q in range(q_y):
                pl.when(y_sends(side, step))(lambda side=side, step=step, q=q: y_copy(side, step, q).wait_send())
                pl.when(y_arrives(side, step))(lambda side=side, step=step, q=q: s_copy(side, step, q).wait_send())
    for q in range(q_y):
        s_copy(0, -1, q).wait_send()


def solution(mesh):
    n_z, n_r = mesh.shape["left"], mesh.shape["right"]
    n_y = n_r // CORES

    def shards(left_act, right_act, counts, w_out):
        rows_l, width_l = left_act.shape
        rows_r, width_r = right_act.shape
        seqs = rows_r * n_z
        left_dev, right_dev = counts.shape
        pair = w_out.shape[1]
        q_z = width_r // 256
        q_y = rows_l // max(128, rows_l // 4)
        lends = n_z == 4 and n_y == 2 and rows_l == rows_r and q_z == 4 and q_y == 4
        extra = [
            pltpu.VMEM((rows_l, width_l), jnp.bfloat16),
            pltpu.VMEM((width_l, rows_l), jnp.bfloat16),
            pltpu.VMEM((q_z, left_dev * right_dev // q_z, pair), jnp.bfloat16),
            pltpu.VMEM((q_z, left_dev * right_dev // q_z, pair), jnp.bfloat16),
            pltpu.VMEM((q_z, left_dev * right_dev // q_z, pair), jnp.float32),
            *[pltpu.SemaphoreType.DMA((2,))] * 4,
            *[pltpu.SemaphoreType.DMA((q_z,))] * 2,
        ]
        projected = pl.pallas_call(
            functools.partial(kernel, (n_z, n_r, q_z, q_y)),
            out_shape=jax.ShapeDtypeStruct((left_dev * right_dev, pair), jnp.float32),
            in_specs=[pl.BlockSpec(memory_space=pltpu.VMEM)] * 3,
            out_specs=pl.BlockSpec(memory_space=pltpu.VMEM),
            scratch_shapes=[
                pltpu.VMEM((seqs, width_l), jnp.bfloat16),
                pltpu.VMEM((seqs, width_r), jnp.bfloat16),
                pltpu.VMEM((width_l, seqs), jnp.bfloat16),
                pltpu.VMEM((width_r // 128, width_l, 128), jnp.float32),
                pltpu.VMEM((width_r // q_z // CH * left_dev, CH * CH), jnp.bfloat16),
                pltpu.SemaphoreType.DMA((2, (n_z - 1) * q_z)),
                pltpu.SemaphoreType.DMA((2, (n_z - 1) * q_z)),
                pltpu.SemaphoreType.DMA((2, (n_y - 1) * q_y)),
                pltpu.SemaphoreType.DMA((2, (n_y - 1) * q_y)),
                pltpu.SemaphoreType.DMA(((2 * n_y - 1) * q_y,)),
                pltpu.SemaphoreType.DMA(((2 * n_y - 1) * q_y,)),
                pltpu.SemaphoreType.DMA,
                *(extra if lends else []),
            ],
            compiler_params=pltpu.CompilerParams(
                collective_id=0, has_side_effects=True, vmem_limit_bytes=56 * 1024 * 1024
            ),
            name="pair_mean",
        )(left_act, right_act, w_out)
        projected = projected.reshape(left_dev, right_dev, pair)
        return projected / counts.astype(jnp.float32)[:, :, None]

    in_specs = (
        P(("groups", "right"), "left"),
        P(("groups", "left"), "right"),
        P(("groups", "left"), "right"),
        P(),
    )
    out_specs = P(("groups", "left"), "right", None)
    return jax.shard_map(shards, mesh=mesh, in_specs=in_specs, out_specs=out_specs, check_vma=False)
```

```python
import functools

import jax
import jax.numpy as jnp
from jax import lax
from jax.experimental import pallas as pl
from jax.experimental.pallas import tpu as pltpu
from jax.sharding import PartitionSpec as P

CH = 32
CORES = 2
MESH = pl.DeviceIdType.MESH


def lane_quads(tiles):
    lane = lax.broadcasted_iota(jnp.int32, tiles[0].shape, 1)
    low = lane < 64
    even = (lane % 64) < 32
    stage = [None] * 4
    for c in range(2):
        a, b = tiles[c], tiles[c + 2]
        stage[c] = jnp.where(low, a, pltpu.roll(b, 64, 1))
        stage[c + 2] = jnp.where(low, pltpu.roll(a, 64, 1), b)
    outs = [None] * 4
    for half in range(2):
        a, b = stage[2 * half], stage[2 * half + 1]
        outs[2 * half] = jnp.where(even, a, pltpu.roll(b, 32, 1))
        outs[2 * half + 1] = jnp.where(even, pltpu.roll(a, 96, 1), b)
    return outs


def kernel(sizes, left_ref, right_ref, counts_ref, w_hbm, out_ref, w_ref, counts_in, cover, out_v, left_full, right_full, left_t, acc, flat,
           z_send, z_recv, y_send, y_recv, s_send, s_recv, own_sem, out_sem):
    n_z, n_r, q_z, q_y = sizes
    n_y = n_r // CORES
    rows_l, width_l = left_ref.shape
    rows_r, width_r = right_ref.shape
    piece_r = width_r // q_z
    piece_l = rows_l // q_y
    left_dev = width_l // CH
    right_dev = width_r // CH
    seqs = left_t.shape[1]
    z = lax.axis_index("left")
    r = lax.axis_index("right")
    y = r // CORES
    k = r % CORES

    def z_dev(pos):
        return {"left": pos}

    def y_dev(pos):
        return {"right": pos * CORES + k}

    sib_dev = {"right": y * CORES + (1 - k)}

    barrier = pltpu.get_barrier_semaphore()

    def greet(dev):
        pl.semaphore_signal(barrier, inc=1, device_id=dev, device_id_type=MESH)

    greet(sib_dev)
    for pos, n, dev in ((z, n_z, z_dev), (y, n_y, y_dev)):
        pl.when(pos + 1 < n)(functools.partial(greet, dev(pos + 1)))
        pl.when(pos >= 1)(functools.partial(greet, dev(pos - 1)))
    total = 1 + (z + 1 < n_z).astype(jnp.int32) + (z >= 1).astype(jnp.int32)
    total = total + (y + 1 < n_y).astype(jnp.int32) + (y >= 1).astype(jnp.int32)
    pl.semaphore_wait(barrier, total)

    def z_slot(chunk, q):
        return right_full.at[pl.ds(pl.multiple_of(chunk * rows_r, rows_r), rows_r), pl.ds(q * piece_r, piece_r)]

    def z_copy(side, step, q):
        sign = 1 - 2 * side
        chunk = z - sign * step
        src = right_ref.at[:, pl.ds(q * piece_r, piece_r)] if step == 0 else z_slot(chunk, q)
        at = step * q_z + q
        return pltpu.make_async_remote_copy(
            src_ref=src, dst_ref=z_slot(chunk, q), send_sem=z_send.at[side, at], recv_sem=z_recv.at[side, at],
            device_id=z_dev(z + sign), device_id_type=MESH)

    def z_sends(side, step):
        near = z + 1 < n_z if side == 0 else z >= 1
        far = z - step >= 0 if side == 0 else z + step < n_z
        return jnp.logical_and(near, far)

    def z_arrives(side, step):
        return z - step - 1 >= 0 if side == 0 else z + step + 1 < n_z

    def z_wait(side, step, q):
        sign = 1 - 2 * side
        slot = z_slot(z - sign * (step + 1), q)
        pltpu.make_async_copy(slot, slot, z_recv.at[side, step * q_z + q]).wait()

    def l_slot(chunk, q):
        return left_full.at[pl.ds(pl.multiple_of(chunk * rows_l + q * piece_l, piece_l), piece_l), :]

    def l_own(q):
        return left_ref.at[pl.ds(q * piece_l, piece_l), :]

    def y_copy(side, step, q):
        sign = 1 - 2 * side
        chunk = (y - sign * step) * CORES + k
        at = step * q_y + q
        return pltpu.make_async_remote_copy(
            src_ref=l_own(q) if step == 0 else l_slot(chunk, q), dst_ref=l_slot(chunk, q),
            send_sem=y_send.at[side, at], recv_sem=y_recv.at[side, at],
            device_id=y_dev(y + sign), device_id_type=MESH)

    def y_sends(side, step):
        near = y + 1 < n_y if side == 0 else y >= 1
        far = y - step >= 0 if side == 0 else y + step < n_y
        return jnp.logical_and(near, far)

    def y_arrives(side, step):
        return y - step - 1 >= 0 if side == 0 else y + step + 1 < n_y

    def y_wait(side, step, q):
        sign = 1 - 2 * side
        slot = l_slot((y - sign * (step + 1)) * CORES + k, q)
        pltpu.make_async_copy(slot, slot, y_recv.at[side, step * q_y + q]).wait()

    def s_at(side, step, q):
        if step < 0:
            return q
        return (1 + side * (n_y - 1) + step) * q_y + q

    def s_copy(side, step, q):
        sign = 1 - 2 * side
        chunk = (y - sign * (step + 1)) * CORES + k if step >= 0 else r
        at = s_at(side, step, q)
        return pltpu.make_async_remote_copy(
            src_ref=l_own(q) if step < 0 else l_slot(chunk, q), dst_ref=l_slot(chunk, q),
            send_sem=s_send.at[at], recv_sem=s_recv.at[at],
            device_id=sib_dev, device_id_type=MESH)

    def s_wait(side, step, q):
        sign = 1 - 2 * side
        y_from = y - sign * (step + 1) if step >= 0 else y
        slot = l_slot(y_from * CORES + (1 - k), q)
        pltpu.make_async_copy(slot, slot, s_recv.at[s_at(side, step, q)]).wait()

    tile = 256

    def turn(src, first_row, chunk, q):
        col = pl.multiple_of(chunk * rows_l + q * piece_l, piece_l)

        def body(m, carry):
            at = pl.multiple_of(m * tile, tile)
            left_t[pl.ds(at, tile), pl.ds(col, piece_l)] = src[pl.ds(first_row, piece_l), pl.ds(at, tile)].T
            return carry

        lax.fori_loop(0, width_l // tile, body, 0)

    def turn_full(chunk, q):
        turn(left_full, pl.multiple_of(chunk * rows_l + q * piece_l, piece_l), chunk, q)

    for q in range(max(q_z, q_y)):
        for side in range(2):
            if q < q_z:
                pl.when(z_sends(side, 0))(lambda side=side, q=q: z_copy(side, 0, q).start())
            if q < q_y:
                pl.when(y_sends(side, 0))(lambda side=side, q=q: y_copy(side, 0, q).start())
    own_left = pltpu.make_async_copy(left_ref, left_full.at[pl.ds(pl.multiple_of(r * rows_l, rows_l), rows_l), :], own_sem.at[0])
    own = pltpu.make_async_copy(right_ref, right_full.at[pl.ds(pl.multiple_of(z * rows_r, rows_r), rows_r), :], own_sem.at[1])
    weights = pltpu.make_async_copy(w_hbm, w_ref, own_sem.at[2])
    counts_copy = pltpu.make_async_copy(counts_ref, counts_in, own_sem.at[3])
    for copy in (own_left, own, weights, counts_copy):
        copy.start()
    for q in range(q_y):
        s_copy(0, -1, q).start()
    own_left.wait()
    for q in range(q_y):
        turn_full(r, q)
    counts_copy.wait()
    counted = counts_in[...].astype(jnp.float32)
    for j in range(right_dev):
        cover[j] = jnp.broadcast_to(counted[:, j:j + 1], (left_dev, cover.shape[2]))
    for q in range(q_y):
        s_wait(0, -1, q)
        turn_full(y * CORES + (1 - k), q)

    def z_tick(step, q):
        for side in range(2):
            @pl.when(z_arrives(side, step))
            def _():
                z_wait(side, step, q)
                if step + 1 < n_z - 1:
                    pl.when(z_sends(side, step + 1))(lambda: z_copy(side, step + 1, q).start())

    def y_tick(step, q):
        for side in range(2):
            @pl.when(y_arrives(side, step))
            def _():
                y_wait(side, step, q)
                s_copy(side, step, q).start()
                if step + 1 < n_y - 1:
                    pl.when(y_sends(side, step + 1))(lambda: y_copy(side, step + 1, q).start())

        for side in range(2):
            @pl.when(y_arrives(side, step))
            def _():
                sign = 1 - 2 * side
                y_from = y - sign * (step + 1)
                turn_full(y_from * CORES + k, q)
                s_wait(side, step, q)
                turn_full(y_from * CORES + (1 - k), q)

    y_ticks = [(step, q) for step in range(n_y - 1) for q in range(q_y)]
    for t in range((n_z - 2) * q_z):
        z_tick(t // q_z, t % q_z)
        if t % 2 == 1 and y_ticks:
            y_tick(*y_ticks.pop(0))
    for tick in y_ticks:
        y_tick(*tick)
    own.wait()
    weights.wait()

    block = 512
    at_end = jnp.logical_or(z == 0, z == n_z - 1)
    base = jnp.where(z == 0, 0, rows_r)
    base = pl.multiple_of(base, rows_r)

    def product(q, first, depth, add):
        cols = pl.ds(q * piece_r, piece_r)

        def body(m, carry):
            rows = pl.ds(pl.multiple_of(m * block, block), block)
            value = jnp.dot(left_t[rows, pl.ds(first, depth)], right_full[pl.ds(first, depth), cols],
                            preferred_element_type=jnp.float32)
            for part in range(piece_r // 128):
                some = value[:, part * 128:(part + 1) * 128]
                slab = q * (piece_r // 128) + part
                acc[slab, rows, :] = acc[slab, rows, :] + some if add else some
            return carry

        lax.fori_loop(0, width_l // block, body, 0)

    def first_part(q):
        @pl.when(at_end)
        def _():
            product(q, base, seqs - rows_r, False)

        @pl.when(jnp.logical_not(at_end))
        def _():
            product(q, 0, seqs, False)

    for q in range(q_z):
        first_part(q)

    def finish(q):
        heads = piece_r // CH
        for quad in range(heads // 4):
            slab = acc.at[q * (piece_r // 128) + quad]
            for cq in range(CH // 4):
                tiles = [slab[pl.ds(cq * 4 + c, left_dev, stride=CH), :].astype(jnp.bfloat16) for c in range(4)]
                for j, value in enumerate(lane_quads(tiles)):
                    flat[pl.ds((quad * 4 + j) * left_dev, left_dev), pl.ds(cq * 128, 128)] = value
        projected = jnp.dot(flat[...], w_ref[...], preferred_element_type=jnp.float32)
        for j in range(heads):
            value = projected[j * left_dev:(j + 1) * left_dev, :] / cover[q * heads + j]
            out_v.at[q].reshape(left_dev * heads, value.shape[1])[pl.ds(j, left_dev, stride=heads), :] = value
        out_copy(q).start()

    def out_copy(q):
        return pltpu.make_async_copy(out_v.at[q], out_ref.at[:, pl.ds(q * heads_q, heads_q), :], out_sem.at[q])

    heads_q = piece_r // CH
    last = n_z - 2
    for q in range(q_z):
        z_tick(last, q)

        @pl.when(at_end)
        def _():
            far = jnp.where(z == 0, (n_z - 1) * rows_r, 0)
            product(q, pl.multiple_of(far, rows_r), rows_r, True)

        finish(q)

    for side in range(2):
        for step in range(n_z - 1):
            for q in range(q_z):
                pl.when(z_sends(side, step))(lambda side=side, step=step, q=q: z_copy(side, step, q).wait_send())
        for step in range(n_y - 1):
            for q in range(q_y):
                pl.when(y_sends(side, step))(lambda side=side, step=step, q=q: y_copy(side, step, q).wait_send())
                pl.when(y_arrives(side, step))(lambda side=side, step=step, q=q: s_copy(side, step, q).wait_send())
    for q in range(q_y):
        s_copy(0, -1, q).wait_send()
    for q in range(q_z):
        out_copy(q).wait()


def solution(mesh):
    n_z, n_r = mesh.shape["left"], mesh.shape["right"]
    n_y = n_r // CORES

    def shards(left_act, right_act, counts, w_out):
        rows_l, width_l = left_act.shape
        rows_r, width_r = right_act.shape
        seqs = rows_r * n_z
        left_dev, right_dev = counts.shape
        pair = w_out.shape[1]
        q_z = width_r // 256
        q_y = rows_l // max(128, rows_l // 4)
        projected = pl.pallas_call(
            functools.partial(kernel, (n_z, n_r, q_z, q_y)),
            out_shape=jax.ShapeDtypeStruct((left_dev, right_dev, pair), jnp.float32),
            in_specs=[pl.BlockSpec(memory_space=pl.ANY)] * 4,
            out_specs=pl.BlockSpec(memory_space=pl.ANY),
            scratch_shapes=[
                pltpu.VMEM(w_out.shape, w_out.dtype),
                pltpu.VMEM(counts.shape, counts.dtype),
                pltpu.VMEM((right_dev, left_dev, pair), jnp.float32),
                pltpu.VMEM((q_z, left_dev, right_dev // q_z, pair), jnp.float32),
                pltpu.VMEM((seqs, width_l), jnp.bfloat16),
                pltpu.VMEM((seqs, width_r), jnp.bfloat16),
                pltpu.VMEM((width_l, seqs), jnp.bfloat16),
                pltpu.VMEM((width_r // 128, width_l, 128), jnp.float32),
                pltpu.VMEM((width_r // q_z // CH * left_dev, CH * CH), jnp.bfloat16),
                pltpu.SemaphoreType.DMA((2, (n_z - 1) * q_z)),
                pltpu.SemaphoreType.DMA((2, (n_z - 1) * q_z)),
                pltpu.SemaphoreType.DMA((2, (n_y - 1) * q_y)),
                pltpu.SemaphoreType.DMA((2, (n_y - 1) * q_y)),
                pltpu.SemaphoreType.DMA(((2 * n_y - 1) * q_y,)),
                pltpu.SemaphoreType.DMA(((2 * n_y - 1) * q_y,)),
                pltpu.SemaphoreType.DMA((4,)),
                pltpu.SemaphoreType.DMA((q_z,)),
            ],
            compiler_params=pltpu.CompilerParams(
                collective_id=0, has_side_effects=True, vmem_limit_bytes=56 * 1024 * 1024
            ),
            name="pair_mean",
        )(left_act, right_act, counts, w_out)
        return projected

    in_specs = (
        P(("groups", "right"), "left"),
        P(("groups", "left"), "right"),
        P(("groups", "left"), "right"),
        P(),
    )
    out_specs = P(("groups", "left"), "right", None)
    return jax.shard_map(shards, mesh=mesh, in_specs=in_specs, out_specs=out_specs, check_vma=False)
```

```python
import functools

import jax
import jax.numpy as jnp
from jax import lax
from jax.experimental import pallas as pl
from jax.experimental.pallas import tpu as pltpu
from jax.sharding import PartitionSpec as P

CH = 32
CORES = 2
MESH = pl.DeviceIdType.MESH


def lane_quads(tiles):
    lane = lax.broadcasted_iota(jnp.int32, tiles[0].shape, 1)
    low = lane < 64
    even = (lane % 64) < 32
    stage = [None] * 4
    for c in range(2):
        a, b = tiles[c], tiles[c + 2]
        stage[c] = jnp.where(low, a, pltpu.roll(b, 64, 1))
        stage[c + 2] = jnp.where(low, pltpu.roll(a, 64, 1), b)
    outs = [None] * 4
    for half in range(2):
        a, b = stage[2 * half], stage[2 * half + 1]
        outs[2 * half] = jnp.where(even, a, pltpu.roll(b, 32, 1))
        outs[2 * half + 1] = jnp.where(even, pltpu.roll(a, 96, 1), b)
    return outs


def kernel(sizes, left_ref, right_ref, counts_ref, w_hbm, out_ref, w_ref, counts_in, cover, out_v, left_full, right_full, left_t, acc, flat,
           z_send, z_recv, y_send, y_recv, s_send, s_recv, own_sem, out_sem):
    n_z, n_r, q_z, q_y = sizes
    n_y = n_r // CORES
    rows_l, width_l = left_ref.shape
    rows_r, width_r = right_ref.shape
    piece_r = width_r // q_z
    piece_l = rows_l // q_y
    left_dev = width_l // CH
    right_dev = width_r // CH
    seqs = left_t.shape[1]
    z = lax.axis_index("left")
    r = lax.axis_index("right")
    y = r // CORES
    k = r % CORES

    def z_dev(pos):
        return {"left": pos}

    def y_dev(pos):
        return {"right": pos * CORES + k}

    sib_dev = {"right": y * CORES + (1 - k)}

    barrier = pltpu.get_barrier_semaphore()

    def greet(dev):
        pl.semaphore_signal(barrier, inc=1, device_id=dev, device_id_type=MESH)

    greet(sib_dev)
    for pos, n, dev in ((z, n_z, z_dev), (y, n_y, y_dev)):
        pl.when(pos + 1 < n)(functools.partial(greet, dev(pos + 1)))
        pl.when(pos >= 1)(functools.partial(greet, dev(pos - 1)))
    total = 1 + (z + 1 < n_z).astype(jnp.int32) + (z >= 1).astype(jnp.int32)
    total = total + (y + 1 < n_y).astype(jnp.int32) + (y >= 1).astype(jnp.int32)
    pl.semaphore_wait(barrier, total)

    def z_slot(chunk, q):
        return right_full.at[pl.ds(pl.multiple_of(chunk * rows_r, rows_r), rows_r), pl.ds(q * piece_r, piece_r)]

    def z_copy(side, step, q):
        sign = 1 - 2 * side
        chunk = z - sign * step
        src = right_ref.at[:, pl.ds(q * piece_r, piece_r)] if step == 0 else z_slot(chunk, q)
        at = step * q_z + q
        return pltpu.make_async_remote_copy(
            src_ref=src, dst_ref=z_slot(chunk, q), send_sem=z_send.at[side, at], recv_sem=z_recv.at[side, at],
            device_id=z_dev(z + sign), device_id_type=MESH)

    def z_sends(side, step):
        near = z + 1 < n_z if side == 0 else z >= 1
        far = z - step >= 0 if side == 0 else z + step < n_z
        return jnp.logical_and(near, far)

    def z_arrives(side, step):
        return z - step - 1 >= 0 if side == 0 else z + step + 1 < n_z

    def z_wait(side, step, q):
        sign = 1 - 2 * side
        slot = z_slot(z - sign * (step + 1), q)
        pltpu.make_async_copy(slot, slot, z_recv.at[side, step * q_z + q]).wait()

    def l_slot(chunk, q):
        return left_full.at[pl.ds(pl.multiple_of(chunk * rows_l + q * piece_l, piece_l), piece_l), :]

    def l_own(q):
        return left_ref.at[pl.ds(q * piece_l, piece_l), :]

    def y_copy(side, step, q):
        sign = 1 - 2 * side
        chunk = (y - sign * step) * CORES + k
        at = step * q_y + q
        return pltpu.make_async_remote_copy(
            src_ref=l_own(q) if step == 0 else l_slot(chunk, q), dst_ref=l_slot(chunk, q),
            send_sem=y_send.at[side, at], recv_sem=y_recv.at[side, at],
            device_id=y_dev(y + sign), device_id_type=MESH)

    def y_sends(side, step):
        near = y + 1 < n_y if side == 0 else y >= 1
        far = y - step >= 0 if side == 0 else y + step < n_y
        return jnp.logical_and(near, far)

    def y_arrives(side, step):
        return y - step - 1 >= 0 if side == 0 else y + step + 1 < n_y

    def y_wait(side, step, q):
        sign = 1 - 2 * side
        slot = l_slot((y - sign * (step + 1)) * CORES + k, q)
        pltpu.make_async_copy(slot, slot, y_recv.at[side, step * q_y + q]).wait()

    def s_at(side, step, q):
        if step < 0:
            return q
        return (1 + side * (n_y - 1) + step) * q_y + q

    def s_copy(side, step, q):
        sign = 1 - 2 * side
        chunk = (y - sign * (step + 1)) * CORES + k if step >= 0 else r
        at = s_at(side, step, q)
        return pltpu.make_async_remote_copy(
            src_ref=l_own(q) if step < 0 else l_slot(chunk, q), dst_ref=l_slot(chunk, q),
            send_sem=s_send.at[at], recv_sem=s_recv.at[at],
            device_id=sib_dev, device_id_type=MESH)

    def s_wait(side, step, q):
        sign = 1 - 2 * side
        y_from = y - sign * (step + 1) if step >= 0 else y
        slot = l_slot(y_from * CORES + (1 - k), q)
        pltpu.make_async_copy(slot, slot, s_recv.at[s_at(side, step, q)]).wait()

    tile = 256

    def turn(src, first_row, chunk, q):
        col = pl.multiple_of(chunk * rows_l + q * piece_l, piece_l)

        def body(m, carry):
            at = pl.multiple_of(m * tile, tile)
            left_t[pl.ds(at, tile), pl.ds(col, piece_l)] = src[pl.ds(first_row, piece_l), pl.ds(at, tile)].T
            return carry

        lax.fori_loop(0, width_l // tile, body, 0)

    def turn_full(chunk, q):
        turn(left_full, pl.multiple_of(chunk * rows_l + q * piece_l, piece_l), chunk, q)

    for q in range(max(q_z, q_y)):
        for side in range(2):
            if q < q_z:
                pl.when(z_sends(side, 0))(lambda side=side, q=q: z_copy(side, 0, q).start())
            if q < q_y:
                pl.when(y_sends(side, 0))(lambda side=side, q=q: y_copy(side, 0, q).start())
    own_left = pltpu.make_async_copy(left_ref, left_full.at[pl.ds(pl.multiple_of(r * rows_l, rows_l), rows_l), :], own_sem.at[0])
    own = pltpu.make_async_copy(right_ref, right_full.at[pl.ds(pl.multiple_of(z * rows_r, rows_r), rows_r), :], own_sem.at[1])
    weights = pltpu.make_async_copy(w_hbm, w_ref, own_sem.at[2])
    counts_copy = pltpu.make_async_copy(counts_ref, counts_in, own_sem.at[3])
    for copy in (own_left, own, weights, counts_copy):
        copy.start()
    for q in range(q_y):
        s_copy(0, -1, q).start()
    own_left.wait()
    for q in range(q_y):
        turn_full(r, q)
    counts_copy.wait()
    counted = counts_in[...].astype(jnp.float32)
    for j in range(right_dev):
        cover[j] = jnp.broadcast_to(counted[:, j:j + 1], (left_dev, cover.shape[2]))
    for q in range(q_y):
        s_wait(0, -1, q)
        turn_full(y * CORES + (1 - k), q)

    def z_tick(step, q):
        for side in range(2):
            @pl.when(z_arrives(side, step))
            def _():
                z_wait(side, step, q)
                if step + 1 < n_z - 1:
                    pl.when(z_sends(side, step + 1))(lambda: z_copy(side, step + 1, q).start())

    def y_tick(step, q):
        for side in range(2):
            @pl.when(y_arrives(side, step))
            def _():
                y_wait(side, step, q)
                s_copy(side, step, q).start()
                if step + 1 < n_y - 1:
                    pl.when(y_sends(side, step + 1))(lambda: y_copy(side, step + 1, q).start())

        for side in range(2):
            @pl.when(y_arrives(side, step))
            def _():
                sign = 1 - 2 * side
                y_from = y - sign * (step + 1)
                turn_full(y_from * CORES + k, q)
                s_wait(side, step, q)
                turn_full(y_from * CORES + (1 - k), q)

    y_ticks = [(step, q) for step in range(n_y - 1) for q in range(q_y)]
    for t in range((n_z - 2) * q_z):
        z_tick(t // q_z, t % q_z)
        if t % 2 == 1 and y_ticks:
            y_tick(*y_ticks.pop(0))
    for tick in y_ticks:
        y_tick(*tick)
    own.wait()
    weights.wait()

    block = 1024
    at_end = jnp.logical_or(z == 0, z == n_z - 1)
    base = jnp.where(z == 0, 0, rows_r)
    base = pl.multiple_of(base, rows_r)

    def product(q, first, depth, add):
        cols = pl.ds(q * piece_r, piece_r)

        def body(m, carry):
            rows = pl.ds(pl.multiple_of(m * block, block), block)
            value = jnp.dot(left_t[rows, pl.ds(first, depth)], right_full[pl.ds(first, depth), cols],
                            preferred_element_type=jnp.float32)
            for part in range(piece_r // 128):
                some = value[:, part * 128:(part + 1) * 128]
                slab = q * (piece_r // 128) + part
                acc[slab, rows, :] = acc[slab, rows, :] + some if add else some
            return carry

        lax.fori_loop(0, width_l // block, body, 0)

    def first_part(q):
        @pl.when(at_end)
        def _():
            product(q, base, seqs - rows_r, False)

        @pl.when(jnp.logical_not(at_end))
        def _():
            product(q, 0, seqs, False)

    for q in range(q_z):
        first_part(q)

    def finish(q):
        heads = piece_r // CH
        for quad in range(heads // 4):
            slab = acc.at[q * (piece_r // 128) + quad]
            for cq in range(CH // 4):
                tiles = [slab[pl.ds(cq * 4 + c, left_dev, stride=CH), :].astype(jnp.bfloat16) for c in range(4)]
                for j, value in enumerate(lane_quads(tiles)):
                    flat[pl.ds((quad * 4 + j) * left_dev, left_dev), pl.ds(cq * 128, 128)] = value
        projected = jnp.dot(flat[...], w_ref[...], preferred_element_type=jnp.float32)
        for j in range(heads):
            value = projected[j * left_dev:(j + 1) * left_dev, :] / cover[q * heads + j]
            out_v.at[q].reshape(left_dev * heads, value.shape[1])[pl.ds(j, left_dev, stride=heads), :] = value
        out_copy(q).start()

    def out_copy(q):
        return pltpu.make_async_copy(out_v.at[q], out_ref.at[:, pl.ds(q * heads_q, heads_q), :], out_sem.at[q])

    heads_q = piece_r // CH
    last = n_z - 2
    for q in range(q_z):
        z_tick(last, q)

        @pl.when(at_end)
        def _():
            far = jnp.where(z == 0, (n_z - 1) * rows_r, 0)
            product(q, pl.multiple_of(far, rows_r), rows_r, True)

        finish(q)

    for side in range(2):
        for step in range(n_z - 1):
            for q in range(q_z):
                pl.when(z_sends(side, step))(lambda side=side, step=step, q=q: z_copy(side, step, q).wait_send())
        for step in range(n_y - 1):
            for q in range(q_y):
                pl.when(y_sends(side, step))(lambda side=side, step=step, q=q: y_copy(side, step, q).wait_send())
                pl.when(y_arrives(side, step))(lambda side=side, step=step, q=q: s_copy(side, step, q).wait_send())
    for q in range(q_y):
        s_copy(0, -1, q).wait_send()
    for q in range(q_z):
        out_copy(q).wait()


def solution(mesh):
    n_z, n_r = mesh.shape["left"], mesh.shape["right"]
    n_y = n_r // CORES

    def shards(left_act, right_act, counts, w_out):
        rows_l, width_l = left_act.shape
        rows_r, width_r = right_act.shape
        seqs = rows_r * n_z
        left_dev, right_dev = counts.shape
        pair = w_out.shape[1]
        q_z = width_r // 256
        q_y = rows_l // max(128, rows_l // 4)
        projected = pl.pallas_call(
            functools.partial(kernel, (n_z, n_r, q_z, q_y)),
            out_shape=jax.ShapeDtypeStruct((left_dev, right_dev, pair), jnp.float32),
            in_specs=[pl.BlockSpec(memory_space=pl.ANY)] * 4,
            out_specs=pl.BlockSpec(memory_space=pl.ANY),
            scratch_shapes=[
                pltpu.VMEM(w_out.shape, w_out.dtype),
                pltpu.VMEM(counts.shape, counts.dtype),
                pltpu.VMEM((right_dev, left_dev, pair), jnp.float32),
                pltpu.VMEM((q_z, left_dev, right_dev // q_z, pair), jnp.float32),
                pltpu.VMEM((seqs, width_l), jnp.bfloat16),
                pltpu.VMEM((seqs, width_r), jnp.bfloat16),
                pltpu.VMEM((width_l, seqs), jnp.bfloat16),
                pltpu.VMEM((width_r // 128, width_l, 128), jnp.float32),
                pltpu.VMEM((width_r // q_z // CH * left_dev, CH * CH), jnp.bfloat16),
                pltpu.SemaphoreType.DMA((2, (n_z - 1) * q_z)),
                pltpu.SemaphoreType.DMA((2, (n_z - 1) * q_z)),
                pltpu.SemaphoreType.DMA((2, (n_y - 1) * q_y)),
                pltpu.SemaphoreType.DMA((2, (n_y - 1) * q_y)),
                pltpu.SemaphoreType.DMA(((2 * n_y - 1) * q_y,)),
                pltpu.SemaphoreType.DMA(((2 * n_y - 1) * q_y,)),
                pltpu.SemaphoreType.DMA((4,)),
                pltpu.SemaphoreType.DMA((q_z,)),
            ],
            compiler_params=pltpu.CompilerParams(
                collective_id=0, has_side_effects=True, vmem_limit_bytes=56 * 1024 * 1024
            ),
            name="pair_mean",
        )(left_act, right_act, counts, w_out)
        return projected

    in_specs = (
        P(("groups", "right"), "left"),
        P(("groups", "left"), "right"),
        P(("groups", "left"), "right"),
        P(),
    )
    out_specs = P(("groups", "left"), "right", None)
    return jax.shard_map(shards, mesh=mesh, in_specs=in_specs, out_specs=out_specs, check_vma=False)
```
